32 devices in a mesh: seq: 8 (over z, core), section: 4 (over y, x).
Axes of the slice: x: 2, y: 2, z: 4, core: 2. Of those that a mesh axis runs over, the one named last changes fastest.
Arguments:
- conv_input: float32 [4, 1024, 256], P('section', 'seq'), may hold values from -6 to 6
- gate: float32 [4, 1024, 256], P('section', 'seq'), may hold values from -6 to 6
- conv_out: float32 [4, 1024, 256], P('section', 'seq'), may hold values from -6 to 6
- incoming: float32 [4, 1024, 256], P('section', 'seq'), may hold values from -6 to 6
- filter_raw: float32 [4, 1024, 256], P('section', 'seq'), may hold values from -6 to 6
- skip_gain: float32 [4, 256], P('section'), may hold values from -4 to 4
- w_value: float32 [4, 256, 256], P('section'), may hold values from -0.375 to 0.375
- w_gate: float32 [4, 256, 256], P('section'), may hold values from -0.375 to 0.375
Outputs:
- handed: float32 [4, 1024, 256], P('section', 'seq')
- filter_grad: float32 [4, 1024, 256], P('section', 'seq')
The draws below stay inside these ranges and needn't reach their ends.
All inputs are finite; a program needn't handle non-finite values.
Results may differ from the reference program's by a relative error of at most 0.000098.
Values sent between devices are 32-bit elements; how exact they have to be, the bound alone decides.
A program may use at most 64 MiB of HBM per device.

```python
import jax
import jax.numpy as jnp
from jax import lax

C = 256
SECTIONS = 4
LEN = 1024


def draw_filter_raw(key, part):
    shape = (SECTIONS, LEN, C)
    return jnp.clip(jax.random.normal(key, shape, jnp.float32), -6.0, 6.0)


def level_of(key, dims, split, least, high):
    def one(position, shards_of):
        heights = jax.random.uniform(jax.random.fold_in(jax.random.fold_in(key, 6), position), (shards_of,), jnp.float32, least / len(split), high / len(split))
        return jnp.repeat(jnp.exp(heights), dims[position] // shards_of).reshape((-1,) + (1,) * (len(dims) - position - 1))

    loudness = one(*split[0])
    for cut in split[1:]:
        loudness = loudness * one(*cut)
    return loudness


def bell_draw(own_key, extent, deviation, reach, split=(), kind=jnp.bfloat16):
    result = jax.random.normal(own_key, extent, jnp.float32) * deviation
    if len(split) > 0:
        result = level_of(own_key, extent, split, -0.22, 0.18) * result
    return jnp.clip(result, min=-reach, max=reach).astype(kind)


def setup_inputs(seed: int = 0) -> dict:
    seeds = jax.random.split(jax.random.key(seed), 9)
    conv_input = bell_draw(seeds[0], (SECTIONS, LEN, C), 1.0, 6.0, ((0, 4), (1, 8)), jnp.float32)
    gate = bell_draw(seeds[1], (SECTIONS, LEN, C), 1.0, 6.0, ((0, 4), (1, 8)), jnp.float32)
    conv_out = bell_draw(seeds[2], (SECTIONS, LEN, C), 1.0, 6.0, ((0, 4), (1, 8)), jnp.float32)
    incoming = bell_draw(seeds[3], (SECTIONS, LEN, C), 1.0, 6.0, ((0, 4), (1, 8)), jnp.float32)
    filter_raw = draw_filter_raw(jax.random.fold_in(seeds[8], 71), 0)
    skip_gain = bell_draw(seeds[5], (SECTIONS, C), 1.0, 4.0, ((0, 4),), jnp.float32)
    w_value = bell_draw(seeds[6], (SECTIONS, C, C), C ** -0.5, 0.375, ((0, 4),), jnp.float32)
    w_gate = bell_draw(seeds[7], (SECTIONS, C, C), C ** -0.5, 0.375, ((0, 4),), jnp.float32)
    return dict(conv_input=conv_input, gate=gate, conv_out=conv_out, incoming=incoming, filter_raw=filter_raw, skip_gain=skip_gain, w_value=w_value, w_gate=w_gate)


exact_mode = lax.Precision.HIGHEST


def section_backward(operands):
    conv_input, gate, conv_out, incoming, filter_raw, skip_gain, w_value, w_gate = operands
    filter_scale = LEN ** -0.5
    kernel = filter_raw * filter_scale
    conv_grad = incoming * gate
    gate_grad = incoming * conv_out
    padded = 2 * LEN
    grad_spec = jnp.fft.rfft(conv_grad, n=padded, axis=0)
    kernel_spec = jnp.fft.rfft(kernel, n=padded, axis=0)
    input_spec = jnp.fft.rfft(conv_input, n=padded, axis=0)
    value_grad = jnp.fft.irfft(jnp.conj(kernel_spec) * grad_spec, n=padded, axis=0)[:LEN]
    filter_grad = jnp.fft.irfft(jnp.conj(input_spec) * grad_spec, n=padded, axis=0)[:LEN]
    value_grad = value_grad.astype(conv_grad.dtype) + skip_gain[None, :] * conv_grad
    input_grad = jnp.dot(value_grad, w_value.T, precision=exact_mode) + jnp.dot(gate_grad, w_gate.T, precision=exact_mode)
    return input_grad, (filter_grad * filter_scale).astype(conv_grad.dtype)


def reference(conv_input, gate, conv_out, incoming, filter_raw, skip_gain, w_value, w_gate):
    input_grad, filter_grad = lax.map(section_backward, (conv_input, gate, conv_out, incoming, filter_raw, skip_gain, w_value, w_gate))
    handed = jnp.roll(input_grad, -1, axis=0)
    return handed, filter_grad
```

```python
import functools

import jax
import jax.numpy as jnp
import numpy as np
from jax import lax
from jax.experimental import pallas as pl
from jax.experimental.pallas import tpu as pltpu
from jax.sharding import PartitionSpec as P

exact_mode = lax.Precision.HIGHEST
full_turn = 6.283185307179586


def passed_along(block, axis, distance):
    devices = range(lax.axis_size(axis))
    route = [((i - distance) % len(devices), i) for i in devices]
    return lax.ppermute(block, axis, route)


def rotations(left_index, right_index, period):
    product = left_index[:, None] * right_index[None, :] % period
    phases = product.astype(jnp.float32) * (full_turn / period)
    return (jnp.cos(phases), jnp.sin(phases))


def across_blocks(signals):
    blocks = signals.shape[1]
    cosine, sine_part = rotations(jnp.arange(2 * blocks), jnp.arange(blocks), 2 * blocks)
    tables = jnp.stack([cosine, -sine_part])
    parts = jnp.einsum("akq,sqrc->askrc", tables, signals, precision=exact_mode)
    return (parts[0], parts[1])


def twiddle(real_part, imag_part, row_index, frequency, period, direction):
    cosine, sine_part = rotations(frequency, row_index, period)
    cosine = cosine[None, :, :, None]
    sine_part = direction * sine_part[None, :, :, None]
    new_real = real_part * cosine + imag_part * sine_part
    new_imag = imag_part * cosine - real_part * sine_part
    return (new_real, new_imag)


def along_rows(real_part, imag_part, direction):
    row_count = real_part.shape[2]
    positions = jnp.arange(row_count)
    cosine, sine_part = rotations(positions, positions, row_count)
    tables = jnp.stack([cosine, direction * sine_part])
    paired = jnp.stack([real_part, imag_part])
    terms = jnp.einsum("ajr,bskrc->abskjc", tables, paired, precision=exact_mode)
    return (terms[0, 0] + terms[1, 1], terms[0, 1] - terms[1, 0])


def inverse_blocks(real_part, imag_part):
    frequency = real_part.shape[1]
    blocks = frequency // 2
    cosine, sine_part = rotations(jnp.arange(blocks), jnp.arange(frequency), frequency)
    first_term = jnp.einsum("qk,skrc->sqrc", cosine, real_part, precision=exact_mode)
    second_term = jnp.einsum("qk,skrc->sqrc", sine_part, imag_part, precision=exact_mode)
    return first_term - second_term


def spectrum_rows(signals):
    devices = lax.axis_size("seq")
    position = lax.axis_index("seq")
    row_count = signals.shape[1]
    slice_rows = row_count // devices
    regrouped = lax.all_to_all(signals, "seq", split_axis=1, concat_axis=1, tiled=True)
    regrouped = regrouped.reshape(signals.shape[0], devices, slice_rows, signals.shape[2])
    real_part, imag_part = across_blocks(regrouped)
    row_index = position * slice_rows + jnp.arange(slice_rows)
    real_part, imag_part = twiddle(
        real_part, imag_part, row_index, jnp.arange(2 * devices), 2 * devices * row_count, 1.0
    )
    complex_pair = lax.all_to_all(
        jnp.stack([real_part, imag_part]), "seq", split_axis=2, concat_axis=3, tiled=True
    )
    return along_rows(complex_pair[0], complex_pair[1], 1.0)


def signal_rows(real_part, imag_part):
    devices = lax.axis_size("seq")
    position = lax.axis_index("seq")
    row_count = real_part.shape[2]
    real_part, imag_part = along_rows(real_part, imag_part, -1.0)
    frequency = position * 2 + jnp.arange(2)
    real_part, imag_part = twiddle(
        real_part, imag_part, jnp.arange(row_count), frequency, 2 * devices * row_count, -1.0
    )
    complex_pair = lax.all_to_all(
        jnp.stack([real_part, imag_part]), "seq", split_axis=3, concat_axis=2, tiled=True
    )
    values = inverse_blocks(complex_pair[0], complex_pair[1])
    regrouped = lax.all_to_all(values, "seq", split_axis=1, concat_axis=2, tiled=True)
    regrouped = regrouped.reshape(values.shape[0], row_count, values.shape[3])
    return regrouped / (2 * devices * row_count)


def correlate(kernel_real, kernel_imag, grad_real, grad_imag):
    product_real = kernel_real * grad_real + kernel_imag * grad_imag
    product_imag = kernel_real * grad_imag - kernel_imag * grad_real
    return (product_real, product_imag)


def spread_out(conv_input, gate, conv_out, incoming, filter_raw, skip_gain, w_value, w_gate):
    row_count = conv_input.shape[1]
    devices = lax.axis_size("seq")
    filter_scale = (devices * row_count) ** (-0.5)
    kernel = filter_raw[0] * filter_scale
    conv_grad = incoming[0] * gate[0]
    gate_grad = incoming[0] * conv_out[0]
    known_real, known_imag = spectrum_rows(jnp.stack([kernel, conv_input[0]]))
    grad_real, grad_imag = spectrum_rows(conv_grad[None])
    product_real, product_imag = correlate(known_real, known_imag, grad_real, grad_imag)
    grads = signal_rows(product_real, product_imag)
    value_grad = grads[0] + skip_gain[0][None, :] * conv_grad
    filter_grad = grads[1] * filter_scale
    input_grad = jnp.einsum("tc,dc->td", value_grad, w_value[0], precision=exact_mode)
    input_grad = input_grad + jnp.einsum("tc,dc->td", gate_grad, w_gate[0], precision=exact_mode)
    handed = passed_along(input_grad, "section", -1)
    return (handed[None], filter_grad[None])


def turn_tables(blocks, rows):
    length = blocks * rows
    angle = 2 * np.pi * (np.outer(np.arange(blocks + 1), np.arange(rows)) % (2 * length)) / (2 * length)
    weight = np.full((blocks + 1, 1), 2.0)
    weight[0] = weight[blocks] = 1.0
    weight = weight * length ** -0.5 / (2 * length)
    turns = np.stack([np.cos(angle), np.sin(angle), np.cos(angle) * weight, np.sin(angle) * weight])
    angle = 2 * np.pi * (np.outer(np.arange(rows), np.arange(rows)) % rows) / rows
    cosine, sine = np.cos(angle), np.sin(angle)
    matrix = np.block([[cosine, -sine], [sine, cosine]]).astype(np.float32)
    return turns.astype(np.float32), matrix


def two_terms(value):
    high = value.astype(jnp.bfloat16)
    return high, (value - high.astype(jnp.float32)).astype(jnp.bfloat16)


def product(left, right, right_dim):
    def dot(a, b):
        return lax.dot_general(a, b, (((1,), (right_dim,)), ((), ())), preferred_element_type=jnp.float32)

    return dot(left[0], right[0]) + (dot(left[1], right[0]) + dot(left[0], right[1]))


def weighted(terms):
    total = None
    for factor, term in terms:
        if abs(factor) < 1e-12:
            continue
        if abs(factor - 1) < 1e-12:
            total = term if total is None else total + term
        elif abs(factor + 1) < 1e-12:
            total = -term if total is None else total - term
        else:
            total = factor * term if total is None else total + factor * term
    return total


def block_spectrum(x):
    blocks = len(x)
    half = blocks // 2
    plus = {p: x[p] + x[blocks - p] for p in range(1, half)}
    minus = {p: x[p] - x[blocks - p] for p in range(1, half)}
    out = []
    for a in range(blocks + 1):
        even, odd = (plus, minus) if a % 2 == 0 else (minus, plus)
        angle = [np.pi * ((p * a) % (2 * blocks)) / blocks for p in range(half + 1)]
        real = [(1.0, x[0])] + [(np.cos(angle[p]), even[p]) for p in range(1, half)]
        real.append((np.cos(angle[half]), x[half]))
        imag = [(-np.sin(angle[p]), odd[p]) for p in range(1, half)]
        imag.append((-np.sin(angle[half]), x[half]))
        out.append((weighted(real), weighted(imag)))
    return out


def block_signal(y):
    blocks = len(y) - 1
    half = blocks // 2
    out = [None] * blocks
    for p in range(half + 1):
        sums = []
        for part, wave in ((0, np.cos), (1, np.sin)):
            for parity in (0, 1):
                sums.append(weighted([
                    (wave(np.pi * ((p * a) % (2 * blocks)) / blocks), y[a][part])
                    for a in range(parity, blocks + 1, 2)
                    if y[a][part] is not None
                ]))
        signs = (1.0, 1.0, -1.0, -1.0)
        out[p] = weighted([(s, v) for s, v in zip(signs, sums) if v is not None])
        if 0 < p < half:
            signs = (1.0, -1.0, 1.0, -1.0)
            out[blocks - p] = weighted([(s, v) for s, v in zip(signs, sums) if v is not None])
    return out


def relay_kernel(
    n, sections,
    x_hbm, gate_hbm, saved_hbm, incoming_hbm, filter_hbm, skip_hbm, wv_hbm, wg_hbm, turn_hbm, matrix_hbm,
    out_ref,
    x_ref, gate_ref, saved_ref, incoming_ref, filter_ref, skip_ref, wv_ref, wg_ref, turn_ref, matrix_ref,
    load_sem,
    source, held, spec, scaled, result, back, passed, received, weight,
    send_sem, recv_sem, back_send, back_recv, hop_send, hop_recv, ready,
):
    me = lax.axis_index("seq")
    section = lax.axis_index("section")
    rows = x_ref.shape[1]
    per = held.shape[2]
    core = lax.rem(me, 2)
    partner = me + 1 - 2 * core
    below = lax.rem(section + sections - 1, sections)
    above = lax.rem(section + 1, sections)

    def other(i):
        return jnp.where(i >= me, i + 1, i)

    pairs = (
        (incoming_hbm, incoming_ref), (gate_hbm, gate_ref), (filter_hbm, filter_ref), (x_hbm, x_ref),
        (saved_hbm, saved_ref), (wg_hbm, wg_ref), (matrix_hbm, matrix_ref), (turn_hbm, turn_ref),
        (wv_hbm, wv_ref), (skip_hbm, skip_ref),
    )
    loads = [pltpu.make_async_copy(src, dst, load_sem.at[i]) for i, (src, dst) in enumerate(pairs)]

    barrier = pltpu.get_barrier_semaphore()

    def tell(semaphore, **to):
        pl.semaphore_signal(semaphore, inc=1, device_id=to, device_id_type=pl.DeviceIdType.MESH)

    for i in range(1, n // 2):
        tell(barrier, seq=lax.rem(me - core + 2 * i, n))
    tell(barrier, seq=partner)
    for i in range(n // 2):
        tell(barrier, seq=2 * i + 1, section=above)
    for load in loads:
        load.start()

    def out_copy(signal, to):
        return pltpu.make_async_remote_copy(
            src_ref=source.at[signal, pl.ds(pl.multiple_of(to * per, 8), per)],
            dst_ref=held.at[signal, me],
            send_sem=send_sem.at[signal, to],
            recv_sem=recv_sem.at[signal, me],
            device_id={"seq": to},
            device_id_type=pl.DeviceIdType.MESH,
        )

    def out_arrival(signal, origin):
        return pltpu.make_async_remote_copy(
            src_ref=source.at[signal, pl.ds(0, per)],
            dst_ref=held.at[signal, origin],
            send_sem=send_sem.at[signal, origin],
            recv_sem=recv_sem.at[signal, origin],
            device_id={"seq": origin},
            device_id_type=pl.DeviceIdType.MESH,
        )

    def back_copy(which, to):
        return pltpu.make_async_remote_copy(
            src_ref=result.at[which, to],
            dst_ref=back.at[which, pl.ds(pl.multiple_of(me * per, 8), per)],
            send_sem=back_send.at[which, to],
            recv_sem=back_recv.at[which, me],
            device_id={"seq": to, "section": section if which else below},
            device_id_type=pl.DeviceIdType.MESH,
        )

    def back_arrival(which, origin):
        return pltpu.make_async_remote_copy(
            src_ref=result.at[which, origin],
            dst_ref=back.at[which, pl.ds(pl.multiple_of(origin * per, 8), per)],
            send_sem=back_send.at[which, origin],
            recv_sem=back_recv.at[which, origin],
            device_id={"seq": origin, "section": section if which else below},
            device_id_type=pl.DeviceIdType.MESH,
        )

    def hop_copy(which, src, dst):
        return pltpu.make_async_remote_copy(
            src_ref=src,
            dst_ref=dst,
            send_sem=hop_send.at[which],
            recv_sem=hop_recv.at[which],
            device_id={"section": below},
            device_id_type=pl.DeviceIdType.MESH,
        )

    weight_hop = hop_copy(0, wv_hbm, weight)
    passed_hop = hop_copy(1, passed, received)
    others = [other(i) for i in range(n - 1)]

    mine = pl.ds(pl.multiple_of(me * per, 8), per)
    for signal in (2, 0, 1):
        if signal == 2:
            loads[0].wait()
            loads[1].wait()
            source[2] = (incoming_ref[0] * gate_ref[0]).T

            @pl.when(core == 0)
            def _():
                pl.semaphore_wait(barrier, n - 1)
                tell(ready, seq=partner)

            @pl.when(core == 1)
            def _():
                pl.semaphore_wait(ready, 1)
        elif signal == 0:
            loads[2].wait()
            source[0] = filter_ref[0].T
        else:
            loads[3].wait()
            source[1] = x_ref[0].T
        for to in others:
            out_copy(signal, to).start()

    @pl.when(core == 1)
    def _():
        pl.semaphore_wait(barrier, n + 1)
        tell(ready, seq=partner)

    @pl.when(core == 0)
    def _():
        pl.semaphore_wait(ready, 1)

    weight_hop.start()
    for signal in range(3):
        held[signal, me] = source[signal, mine]

    for load in loads[4:]:
        load.wait()
    passed[...] = product(two_terms(incoming_ref[0] * saved_ref[0]), two_terms(wg_ref[0]), 1) + product(
        two_terms(skip_ref[...] * (incoming_ref[0] * gate_ref[0])), two_terms(wv_ref[0]), 1
    )
    passed_hop.start()
    matrix = two_terms(matrix_ref[...])

    def forward(signal):
        for origin in others:
            out_arrival(signal, origin).wait_recv()
        for a, (real, imag) in enumerate(block_spectrum([held[signal, p] for p in range(n)])):
            at = pl.ds(a * per, per)
            if a == 0:
                scaled[at, :rows] = real
                scaled[at, rows:] = jnp.zeros_like(real)
                continue
            cosine, sine = turn_ref[0, a : a + 1], turn_ref[1, a : a + 1]
            if imag is None:
                scaled[at, :rows] = real * cosine
                scaled[at, rows:] = -real * sine
            else:
                scaled[at, :rows] = real * cosine + imag * sine
                scaled[at, rows:] = imag * cosine - real * sine
        spec[signal] = product(two_terms(scaled[...]), matrix, 0)

    def inverse(which):
        kr, ki = spec[which, :, :rows], spec[which, :, rows:]
        gr, gi = spec[2, :, :rows], spec[2, :, rows:]
        scaled[:, :rows] = kr * gr + ki * gi
        scaled[:, rows:] = kr * gi - ki * gr
        scaled[...] = product(two_terms(scaled[...]), matrix, 1)
        terms = []
        for a in range(n + 1):
            at = pl.ds(a * per, per)
            real, imag = scaled[at, :rows], scaled[at, rows:]
            cosine, sine = turn_ref[2, a : a + 1], turn_ref[3, a : a + 1]
            if a == 0:
                terms.append((real * cosine, None))
            elif a == n:
                terms.append((real * cosine - imag * sine, None))
            else:
                terms.append((real * cosine - imag * sine, real * sine + imag * cosine))
        for p, value in enumerate(block_signal(terms)):
            result[which, p] = value
        for to in others if which else range(n):
            back_copy(which, to).start()

    forward(2)
    forward(0)
    inverse(0)
    forward(1)
    inverse(1)

    back[1, mine] = result[1, me]
    weight_hop.wait_recv()
    passed_hop.wait_recv()
    w_above = two_terms(weight[0])
    for origin in range(n):
        back_arrival(0, origin).wait_recv()
    out_ref[0] = product(two_terms(back[0].T), w_above, 1) + received[...]
    for origin in others:
        back_arrival(1, origin).wait_recv()
    out_ref[1] = back[1].T
    for to in others:
        for signal in range(3):
            out_copy(signal, to).wait_send()
        back_copy(1, to).wait_send()
    for to in range(n):
        back_copy(0, to).wait_send()
    weight_hop.wait_send()
    passed_hop.wait_send()


def in_one_kernel(*operands):
    n, sections = lax.axis_size("seq"), lax.axis_size("section")
    _, rows, channels = operands[0].shape
    per = channels // n
    turns, matrix = turn_tables(n, rows)
    vmem = pl.BlockSpec(memory_space=pltpu.VMEM)
    shape = pltpu.VMEM(operands[0].shape, jnp.float32)
    spectrum = ((n + 1) * per, 2 * rows)
    dma = pltpu.SemaphoreType.DMA
    return pl.pallas_call(
        functools.partial(relay_kernel, n, sections),
        out_shape=pltpu.VMEM((2,) + operands[0].shape[1:], jnp.float32),
        in_specs=[pl.BlockSpec(memory_space=pltpu.HBM)] * 10,
        out_specs=vmem,
        scratch_shapes=[
            *(pltpu.VMEM(operand.shape, jnp.float32) for operand in operands + (turns, matrix)),
            dma((10,)),
            pltpu.VMEM((3, channels, rows), jnp.float32),
            pltpu.VMEM((3, n, per, rows), jnp.float32),
            pltpu.VMEM((3,) + spectrum, jnp.float32),
            pltpu.VMEM(spectrum, jnp.float32),
            pltpu.VMEM((2, n, per, rows), jnp.float32),
            pltpu.VMEM((2, channels, rows), jnp.float32),
            pltpu.VMEM((rows, channels), jnp.float32),
            pltpu.VMEM((rows, channels), jnp.float32),
            pltpu.VMEM((1, channels, channels), jnp.float32),
            dma((3, n)), dma((3, n)),
            dma((2, n)), dma((2, n)),
            dma((2,)), dma((2,)),
            pltpu.SemaphoreType.REGULAR,
        ],
        compiler_params=pltpu.CompilerParams(
            collective_id=0, has_side_effects=True, vmem_limit_bytes=60 * 2**20
        ),
    )(*operands, turns, matrix)


def per_device(*operands):
    n, sections = lax.axis_size("seq"), lax.axis_size("section")
    _, rows, channels = operands[0].shape
    if sections > 1 and channels % (8 * n) == 0 and n % 2 == 0 and rows % 128 == 0:
        both = in_one_kernel(*operands)
        return both[:1], both[1:]
    return spread_out(*operands)


def solution(mesh):
    in_specs = (
        P("section", "seq", None),
        P("section", "seq", None),
        P("section", "seq", None),
        P("section", "seq", None),
        P("section", "seq", None),
        P("section", None),
        P("section", None, None),
        P("section", None, None),
    )
    out_specs = (P("section", "seq", None), P("section", "seq", None))
    return jax.shard_map(
        per_device, mesh=mesh, in_specs=in_specs, out_specs=out_specs, check_vma=False
    )
```

```python
import functools

import jax
import jax.numpy as jnp
import numpy as np
from jax import lax
from jax.experimental import pallas as pl
from jax.experimental.pallas import tpu as pltpu
from jax.sharding import PartitionSpec as P

exact_mode = lax.Precision.HIGHEST
full_turn = 6.283185307179586


def passed_along(block, axis, distance):
    devices = range(lax.axis_size(axis))
    route = [((i - distance) % len(devices), i) for i in devices]
    return lax.ppermute(block, axis, route)


def rotations(left_index, right_index, period):
    product = left_index[:, None] * right_index[None, :] % period
    phases = product.astype(jnp.float32) * (full_turn / period)
    return (jnp.cos(phases), jnp.sin(phases))


def across_blocks(signals):
    blocks = signals.shape[1]
    cosine, sine_part = rotations(jnp.arange(2 * blocks), jnp.arange(blocks), 2 * blocks)
    tables = jnp.stack([cosine, -sine_part])
    parts = jnp.einsum("akq,sqrc->askrc", tables, signals, precision=exact_mode)
    return (parts[0], parts[1])


def twiddle(real_part, imag_part, row_index, frequency, period, direction):
    cosine, sine_part = rotations(frequency, row_index, period)
    cosine = cosine[None, :, :, None]
    sine_part = direction * sine_part[None, :, :, None]
    new_real = real_part * cosine + imag_part * sine_part
    new_imag = imag_part * cosine - real_part * sine_part
    return (new_real, new_imag)


def along_rows(real_part, imag_part, direction):
    row_count = real_part.shape[2]
    positions = jnp.arange(row_count)
    cosine, sine_part = rotations(positions, positions, row_count)
    tables = jnp.stack([cosine, direction * sine_part])
    paired = jnp.stack([real_part, imag_part])
    terms = jnp.einsum("ajr,bskrc->abskjc", tables, paired, precision=exact_mode)
    return (terms[0, 0] + terms[1, 1], terms[0, 1] - terms[1, 0])


def inverse_blocks(real_part, imag_part):
    frequency = real_part.shape[1]
    blocks = frequency // 2
    cosine, sine_part = rotations(jnp.arange(blocks), jnp.arange(frequency), frequency)
    first_term = jnp.einsum("qk,skrc->sqrc", cosine, real_part, precision=exact_mode)
    second_term = jnp.einsum("qk,skrc->sqrc", sine_part, imag_part, precision=exact_mode)
    return first_term - second_term


def spectrum_rows(signals):
    devices = lax.axis_size("seq")
    position = lax.axis_index("seq")
    row_count = signals.shape[1]
    slice_rows = row_count // devices
    regrouped = lax.all_to_all(signals, "seq", split_axis=1, concat_axis=1, tiled=True)
    regrouped = regrouped.reshape(signals.shape[0], devices, slice_rows, signals.shape[2])
    real_part, imag_part = across_blocks(regrouped)
    row_index = position * slice_rows + jnp.arange(slice_rows)
    real_part, imag_part = twiddle(
        real_part, imag_part, row_index, jnp.arange(2 * devices), 2 * devices * row_count, 1.0
    )
    complex_pair = lax.all_to_all(
        jnp.stack([real_part, imag_part]), "seq", split_axis=2, concat_axis=3, tiled=True
    )
    return along_rows(complex_pair[0], complex_pair[1], 1.0)


def signal_rows(real_part, imag_part):
    devices = lax.axis_size("seq")
    position = lax.axis_index("seq")
    row_count = real_part.shape[2]
    real_part, imag_part = along_rows(real_part, imag_part, -1.0)
    frequency = position * 2 + jnp.arange(2)
    real_part, imag_part = twiddle(
        real_part, imag_part, jnp.arange(row_count), frequency, 2 * devices * row_count, -1.0
    )
    complex_pair = lax.all_to_all(
        jnp.stack([real_part, imag_part]), "seq", split_axis=3, concat_axis=2, tiled=True
    )
    values = inverse_blocks(complex_pair[0], complex_pair[1])
    regrouped = lax.all_to_all(values, "seq", split_axis=1, concat_axis=2, tiled=True)
    regrouped = regrouped.reshape(values.shape[0], row_count, values.shape[3])
    return regrouped / (2 * devices * row_count)


def correlate(kernel_real, kernel_imag, grad_real, grad_imag):
    product_real = kernel_real * grad_real + kernel_imag * grad_imag
    product_imag = kernel_real * grad_imag - kernel_imag * grad_real
    return (product_real, product_imag)


def spread_out(conv_input, gate, conv_out, incoming, filter_raw, skip_gain, w_value, w_gate):
    row_count = conv_input.shape[1]
    devices = lax.axis_size("seq")
    filter_scale = (devices * row_count) ** (-0.5)
    kernel = filter_raw[0] * filter_scale
    conv_grad = incoming[0] * gate[0]
    gate_grad = incoming[0] * conv_out[0]
    known_real, known_imag = spectrum_rows(jnp.stack([kernel, conv_input[0]]))
    grad_real, grad_imag = spectrum_rows(conv_grad[None])
    product_real, product_imag = correlate(known_real, known_imag, grad_real, grad_imag)
    grads = signal_rows(product_real, product_imag)
    value_grad = grads[0] + skip_gain[0][None, :] * conv_grad
    filter_grad = grads[1] * filter_scale
    input_grad = jnp.einsum("tc,dc->td", value_grad, w_value[0], precision=exact_mode)
    input_grad = input_grad + jnp.einsum("tc,dc->td", gate_grad, w_gate[0], precision=exact_mode)
    handed = passed_along(input_grad, "section", -1)
    return (handed[None], filter_grad[None])


def turn_tables(blocks, rows):
    length = blocks * rows
    angle = 2 * np.pi * (np.outer(np.arange(blocks + 1), np.arange(rows)) % (2 * length)) / (2 * length)
    weight = np.full((blocks + 1, 1), 2.0)
    weight[0] = weight[blocks] = 1.0
    weight = weight * length ** -0.5 / (2 * length)
    turns = np.stack([np.cos(angle), np.sin(angle), np.cos(angle) * weight, np.sin(angle) * weight])
    angle = 2 * np.pi * (np.outer(np.arange(rows), np.arange(rows)) % rows) / rows
    cosine, sine = np.cos(angle), np.sin(angle)
    matrix = np.block([[cosine, -sine], [sine, cosine]]).astype(np.float32)
    return turns.astype(np.float32), matrix


def two_terms(value):
    high = value.astype(jnp.bfloat16)
    return high, (value - high.astype(jnp.float32)).astype(jnp.bfloat16)


def product(left, right, right_dim):
    def dot(a, b):
        return lax.dot_general(a, b, (((1,), (right_dim,)), ((), ())), preferred_element_type=jnp.float32)

    return dot(left[0], right[0]) + (dot(left[1], right[0]) + dot(left[0], right[1]))


def weighted(terms):
    total = None
    for factor, term in terms:
        if abs(factor) < 1e-12:
            continue
        if abs(factor - 1) < 1e-12:
            total = term if total is None else total + term
        elif abs(factor + 1) < 1e-12:
            total = -term if total is None else total - term
        else:
            total = factor * term if total is None else total + factor * term
    return total


def block_spectrum(x):
    blocks = len(x)
    half = blocks // 2
    plus = {p: x[p] + x[blocks - p] for p in range(1, half)}
    minus = {p: x[p] - x[blocks - p] for p in range(1, half)}
    out = []
    for a in range(blocks + 1):
        even, odd = (plus, minus) if a % 2 == 0 else (minus, plus)
        angle = [np.pi * ((p * a) % (2 * blocks)) / blocks for p in range(half + 1)]
        real = [(1.0, x[0])] + [(np.cos(angle[p]), even[p]) for p in range(1, half)]
        real.append((np.cos(angle[half]), x[half]))
        imag = [(-np.sin(angle[p]), odd[p]) for p in range(1, half)]
        imag.append((-np.sin(angle[half]), x[half]))
        out.append((weighted(real), weighted(imag)))
    return out


def block_signal(y):
    blocks = len(y) - 1
    half = blocks // 2
    out = [None] * blocks
    for p in range(half + 1):
        sums = []
        for part, wave in ((0, np.cos), (1, np.sin)):
            for parity in (0, 1):
                sums.append(weighted([
                    (wave(np.pi * ((p * a) % (2 * blocks)) / blocks), y[a][part])
                    for a in range(parity, blocks + 1, 2)
                    if y[a][part] is not None
                ]))
        signs = (1.0, 1.0, -1.0, -1.0)
        out[p] = weighted([(s, v) for s, v in zip(signs, sums) if v is not None])
        if 0 < p < half:
            signs = (1.0, -1.0, 1.0, -1.0)
            out[blocks - p] = weighted([(s, v) for s, v in zip(signs, sums) if v is not None])
    return out


def relay_kernel(
    n, sections,
    x_hbm, gate_hbm, saved_hbm, incoming_hbm, filter_hbm, skip_hbm, wv_hbm, wg_hbm, turn_hbm, matrix_hbm,
    out_ref,
    x_ref, gate_ref, saved_ref, incoming_ref, filter_ref, skip_ref, wv_ref, wg_ref, turn_ref, matrix_ref,
    load_sem,
    source, held, spec, scaled, result, back, passed, received, weight,
    send_sem, recv_sem, back_send, back_recv, hop_send, hop_recv, ready,
):
    me = lax.axis_index("seq")
    section = lax.axis_index("section")
    rows = x_ref.shape[1]
    per = held.shape[2]
    core = lax.rem(me, 2)
    partner = me + 1 - 2 * core
    below = lax.rem(section + sections - 1, sections)
    above = lax.rem(section + 1, sections)

    chip = me // 2
    first = n // 4 + 1
    early = (chip < first).astype(jnp.int32)

    pairs = (
        (incoming_hbm, incoming_ref), (gate_hbm, gate_ref), (filter_hbm, filter_ref), (x_hbm, x_ref),
        (saved_hbm, saved_ref), (wg_hbm, wg_ref), (matrix_hbm, matrix_ref), (turn_hbm, turn_ref),
        (wv_hbm, wv_ref), (skip_hbm, skip_ref),
    )
    loads = [pltpu.make_async_copy(src, dst, load_sem.at[i]) for i, (src, dst) in enumerate(pairs)]

    barrier = pltpu.get_barrier_semaphore()

    def tell(semaphore, **to):
        pl.semaphore_signal(semaphore, inc=1, device_id=to, device_id_type=pl.DeviceIdType.MESH)

    for i in range(1, n // 2):
        tell(barrier, seq=2 * lax.rem(chip + i, n // 2) + 1 - early)
    tell(barrier, seq=partner)
    for neighbour in (below, above):
        tell(barrier, seq=2 * chip + 1, section=neighbour)
    for load in loads:
        load.start()

    def hear_first():
        @pl.when(core == 0)
        def _():
            pl.semaphore_wait(barrier, 2 * (first - early) + 1)
            tell(ready.at[0], seq=partner)

        @pl.when(core == 1)
        def _():
            pl.semaphore_wait(ready.at[0], 1)

    def hear_rest():
        @pl.when(core == 1)
        def _():
            pl.semaphore_wait(barrier, 2 * (n // 2 - first - 1 + early) + 5)
            tell(ready.at[1], seq=partner)
            tell(ready.at[2], seq=me, section=above)
            tell(ready.at[2], seq=partner, section=above)

        @pl.when(core == 0)
        def _():
            pl.semaphore_wait(ready.at[1], 1)

    def each(places, act):
        for p in places:
            pl.when(p != me)(functools.partial(act, p))

    def out_copy(signal, to):
        return pltpu.make_async_remote_copy(
            src_ref=source.at[signal, pl.ds(pl.multiple_of(to * per, 8), per)],
            dst_ref=held.at[signal, me],
            send_sem=send_sem.at[signal, to],
            recv_sem=recv_sem.at[signal, me],
            device_id={"seq": to},
            device_id_type=pl.DeviceIdType.MESH,
        )

    def out_arrival(signal, origin):
        return pltpu.make_async_remote_copy(
            src_ref=source.at[signal, pl.ds(0, per)],
            dst_ref=held.at[signal, origin],
            send_sem=send_sem.at[signal, origin],
            recv_sem=recv_sem.at[signal, origin],
            device_id={"seq": origin},
            device_id_type=pl.DeviceIdType.MESH,
        )

    def back_copy(which, to):
        return pltpu.make_async_remote_copy(
            src_ref=result.at[which, to],
            dst_ref=back.at[which, pl.ds(pl.multiple_of(me * per, 8), per)],
            send_sem=back_send.at[which, to],
            recv_sem=back_recv.at[which, me],
            device_id={"seq": to, "section": section if which else below},
            device_id_type=pl.DeviceIdType.MESH,
        )

    def back_arrival(which, origin):
        return pltpu.make_async_remote_copy(
            src_ref=result.at[which, origin],
            dst_ref=back.at[which, pl.ds(pl.multiple_of(origin * per, 8), per)],
            send_sem=back_send.at[which, origin],
            recv_sem=back_recv.at[which, origin],
            device_id={"seq": origin, "section": section if which else below},
            device_id_type=pl.DeviceIdType.MESH,
        )

    def hop_copy(which, src, dst):
        return pltpu.make_async_remote_copy(
            src_ref=src,
            dst_ref=dst,
            send_sem=hop_send.at[which],
            recv_sem=hop_recv.at[which],
            device_id={"section": below},
            device_id_type=pl.DeviceIdType.MESH,
        )

    weight_hop = hop_copy(0, wv_hbm, weight)
    passed_hop = hop_copy(1, passed, received)
    mine = pl.ds(pl.multiple_of(me * per, 8), per)
    soon, late = range(2 * first), range(2 * first, n)

    def send(signal, places):
        each(places, lambda to: out_copy(signal, to).start())

    loads[0].wait()
    loads[1].wait()
    source[2] = (incoming_ref[0] * gate_ref[0]).T
    hear_first()
    send(2, soon)
    loads[2].wait()
    source[0] = filter_ref[0].T
    send(0, soon)
    loads[3].wait()
    source[1] = x_ref[0].T
    hear_rest()
    send(2, late)
    send(0, late)
    send(1, range(n))
    weight_hop.start()
    for signal in range(3):
        held[signal, me] = source[signal, mine]

    for load in loads[4:]:
        load.wait()
    passed[...] = product(two_terms(incoming_ref[0] * saved_ref[0]), two_terms(wg_ref[0]), 1) + product(
        two_terms(skip_ref[...] * (incoming_ref[0] * gate_ref[0])), two_terms(wv_ref[0]), 1
    )
    passed_hop.start()
    matrix = two_terms(matrix_ref[...])

    def forward(signal):
        each(range(n), lambda origin: out_arrival(signal, origin).wait_recv())
        for a, (real, imag) in enumerate(block_spectrum([held[signal, p] for p in range(n)])):
            at = pl.ds(a * per, per)
            if a == 0:
                scaled[at, :rows] = real
                scaled[at, rows:] = jnp.zeros_like(real)
                continue
            cosine, sine = turn_ref[0, a : a + 1], turn_ref[1, a : a + 1]
            if imag is None:
                scaled[at, :rows] = real * cosine
                scaled[at, rows:] = -real * sine
            else:
                scaled[at, :rows] = real * cosine + imag * sine
                scaled[at, rows:] = imag * cosine - real * sine
        spec[signal] = product(two_terms(scaled[...]), matrix, 0)

    def inverse(which):
        kr, ki = spec[which, :, :rows], spec[which, :, rows:]
        gr, gi = spec[2, :, :rows], spec[2, :, rows:]
        scaled[:, :rows] = kr * gr + ki * gi
        scaled[:, rows:] = kr * gi - ki * gr
        scaled[...] = product(two_terms(scaled[...]), matrix, 1)
        terms = []
        for a in range(n + 1):
            at = pl.ds(a * per, per)
            real, imag = scaled[at, :rows], scaled[at, rows:]
            cosine, sine = turn_ref[2, a : a + 1], turn_ref[3, a : a + 1]
            if a == 0:
                terms.append((real * cosine, None))
            elif a == n:
                terms.append((real * cosine - imag * sine, None))
            else:
                terms.append((real * cosine - imag * sine, real * sine + imag * cosine))
        for p, value in enumerate(block_signal(terms)):
            result[which, p] = value
        if which:
            each(range(n), lambda to: back_copy(1, to).start())
        else:
            pl.semaphore_wait(ready.at[2], 1)
            for to in range(n):
                back_copy(0, to).start()

    forward(2)
    forward(0)
    inverse(0)
    forward(1)
    inverse(1)

    back[1, mine] = result[1, me]
    weight_hop.wait_recv()
    passed_hop.wait_recv()
    w_above = two_terms(weight[0])
    for origin in range(n):
        back_arrival(0, origin).wait_recv()
    out_ref[0] = product(two_terms(back[0].T), w_above, 1) + received[...]
    each(range(n), lambda origin: back_arrival(1, origin).wait_recv())
    out_ref[1] = back[1].T
    for signal in range(3):
        each(range(n), lambda to: out_copy(signal, to).wait_send())
    each(range(n), lambda to: back_copy(1, to).wait_send())
    for to in range(n):
        back_copy(0, to).wait_send()
    weight_hop.wait_send()
    passed_hop.wait_send()


def in_one_kernel(*operands):
    n, sections = lax.axis_size("seq"), lax.axis_size("section")
    _, rows, channels = operands[0].shape
    per = channels // n
    turns, matrix = turn_tables(n, rows)
    vmem = pl.BlockSpec(memory_space=pltpu.VMEM)
    shape = pltpu.VMEM(operands[0].shape, jnp.float32)
    spectrum = ((n + 1) * per, 2 * rows)
    dma = pltpu.SemaphoreType.DMA
    return pl.pallas_call(
        functools.partial(relay_kernel, n, sections),
        out_shape=pltpu.VMEM((2,) + operands[0].shape[1:], jnp.float32),
        in_specs=[pl.BlockSpec(memory_space=pltpu.HBM)] * 10,
        out_specs=vmem,
        scratch_shapes=[
            *(pltpu.VMEM(operand.shape, jnp.float32) for operand in operands + (turns, matrix)),
            dma((10,)),
            pltpu.VMEM((3, channels, rows), jnp.float32),
            pltpu.VMEM((3, n, per, rows), jnp.float32),
            pltpu.VMEM((3,) + spectrum, jnp.float32),
            pltpu.VMEM(spectrum, jnp.float32),
            pltpu.VMEM((2, n, per, rows), jnp.float32),
            pltpu.VMEM((2, channels, rows), jnp.float32),
            pltpu.VMEM((rows, channels), jnp.float32),
            pltpu.VMEM((rows, channels), jnp.float32),
            pltpu.VMEM((1, channels, channels), jnp.float32),
            dma((3, n)), dma((3, n)),
            dma((2, n)), dma((2, n)),
            dma((2,)), dma((2,)),
            pltpu.SemaphoreType.REGULAR((3,)),
        ],
        compiler_params=pltpu.CompilerParams(
            collective_id=0, has_side_effects=True, vmem_limit_bytes=60 * 2**20
        ),
    )(*operands, turns, matrix)


def per_device(*operands):
    n, sections = lax.axis_size("seq"), lax.axis_size("section")
    _, rows, channels = operands[0].shape
    if sections > 1 and channels % (8 * n) == 0 and n % 2 == 0 and rows % 128 == 0:
        both = in_one_kernel(*operands)
        return both[:1], both[1:]
    return spread_out(*operands)


def solution(mesh):
    in_specs = (
        P("section", "seq", None),
        P("section", "seq", None),
        P("section", "seq", None),
        P("section", "seq", None),
        P("section", "seq", None),
        P("section", None),
        P("section", None, None),
        P("section", None, None),
    )
    out_specs = (P("section", "seq", None), P("section", "seq", None))
    return jax.shard_map(
        per_device, mesh=mesh, in_specs=in_specs, out_specs=out_specs, check_vma=False
    )
```

```python
import functools

import jax
import jax.numpy as jnp
import numpy as np
from jax import lax
from jax.experimental import pallas as pl
from jax.experimental.pallas import tpu as pltpu
from jax.sharding import PartitionSpec as P

exact_mode = lax.Precision.HIGHEST
full_turn = 6.283185307179586


def passed_along(block, axis, distance):
    devices = range(lax.axis_size(axis))
    route = [((i - distance) % len(devices), i) for i in devices]
    return lax.ppermute(block, axis, route)


def rotations(left_index, right_index, period):
    product = left_index[:, None] * right_index[None, :] % period
    phases = product.astype(jnp.float32) * (full_turn / period)
    return (jnp.cos(phases), jnp.sin(phases))


def across_blocks(signals):
    blocks = signals.shape[1]
    cosine, sine_part = rotations(jnp.arange(2 * blocks), jnp.arange(blocks), 2 * blocks)
    tables = jnp.stack([cosine, -sine_part])
    parts = jnp.einsum("akq,sqrc->askrc", tables, signals, precision=exact_mode)
    return (parts[0], parts[1])


def twiddle(real_part, imag_part, row_index, frequency, period, direction):
    cosine, sine_part = rotations(frequency, row_index, period)
    cosine = cosine[None, :, :, None]
    sine_part = direction * sine_part[None, :, :, None]
    new_real = real_part * cosine + imag_part * sine_part
    new_imag = imag_part * cosine - real_part * sine_part
    return (new_real, new_imag)


def along_rows(real_part, imag_part, direction):
    row_count = real_part.shape[2]
    positions = jnp.arange(row_count)
    cosine, sine_part = rotations(positions, positions, row_count)
    tables = jnp.stack([cosine, direction * sine_part])
    paired = jnp.stack([real_part, imag_part])
    terms = jnp.einsum("ajr,bskrc->abskjc", tables, paired, precision=exact_mode)
    return (terms[0, 0] + terms[1, 1], terms[0, 1] - terms[1, 0])


def inverse_blocks(real_part, imag_part):
    frequency = real_part.shape[1]
    blocks = frequency // 2
    cosine, sine_part = rotations(jnp.arange(blocks), jnp.arange(frequency), frequency)
    first_term = jnp.einsum("qk,skrc->sqrc", cosine, real_part, precision=exact_mode)
    second_term = jnp.einsum("qk,skrc->sqrc", sine_part, imag_part, precision=exact_mode)
    return first_term - second_term


def spectrum_rows(signals):
    devices = lax.axis_size("seq")
    position = lax.axis_index("seq")
    row_count = signals.shape[1]
    slice_rows = row_count // devices
    regrouped = lax.all_to_all(signals, "seq", split_axis=1, concat_axis=1, tiled=True)
    regrouped = regrouped.reshape(signals.shape[0], devices, slice_rows, signals.shape[2])
    real_part, imag_part = across_blocks(regrouped)
    row_index = position * slice_rows + jnp.arange(slice_rows)
    real_part, imag_part = twiddle(
        real_part, imag_part, row_index, jnp.arange(2 * devices), 2 * devices * row_count, 1.0
    )
    complex_pair = lax.all_to_all(
        jnp.stack([real_part, imag_part]), "seq", split_axis=2, concat_axis=3, tiled=True
    )
    return along_rows(complex_pair[0], complex_pair[1], 1.0)


def signal_rows(real_part, imag_part):
    devices = lax.axis_size("seq")
    position = lax.axis_index("seq")
    row_count = real_part.shape[2]
    real_part, imag_part = along_rows(real_part, imag_part, -1.0)
    frequency = position * 2 + jnp.arange(2)
    real_part, imag_part = twiddle(
        real_part, imag_part, jnp.arange(row_count), frequency, 2 * devices * row_count, -1.0
    )
    complex_pair = lax.all_to_all(
        jnp.stack([real_part, imag_part]), "seq", split_axis=3, concat_axis=2, tiled=True
    )
    values = inverse_blocks(complex_pair[0], complex_pair[1])
    regrouped = lax.all_to_all(values, "seq", split_axis=1, concat_axis=2, tiled=True)
    regrouped = regrouped.reshape(values.shape[0], row_count, values.shape[3])
    return regrouped / (2 * devices * row_count)


def correlate(kernel_real, kernel_imag, grad_real, grad_imag):
    product_real = kernel_real * grad_real + kernel_imag * grad_imag
    product_imag = kernel_real * grad_imag - kernel_imag * grad_real
    return (product_real, product_imag)


def spread_out(conv_input, gate, conv_out, incoming, filter_raw, skip_gain, w_value, w_gate):
    row_count = conv_input.shape[1]
    devices = lax.axis_size("seq")
    filter_scale = (devices * row_count) ** (-0.5)
    kernel = filter_raw[0] * filter_scale
    conv_grad = incoming[0] * gate[0]
    gate_grad = incoming[0] * conv_out[0]
    known_real, known_imag = spectrum_rows(jnp.stack([kernel, conv_input[0]]))
    grad_real, grad_imag = spectrum_rows(conv_grad[None])
    product_real, product_imag = correlate(known_real, known_imag, grad_real, grad_imag)
    grads = signal_rows(product_real, product_imag)
    value_grad = grads[0] + skip_gain[0][None, :] * conv_grad
    filter_grad = grads[1] * filter_scale
    input_grad = jnp.einsum("tc,dc->td", value_grad, w_value[0], precision=exact_mode)
    input_grad = input_grad + jnp.einsum("tc,dc->td", gate_grad, w_gate[0], precision=exact_mode)
    handed = passed_along(input_grad, "section", -1)
    return (handed[None], filter_grad[None])


def turn_tables(blocks, rows):
    length = blocks * rows
    angle = 2 * np.pi * (np.outer(np.arange(blocks + 1), np.arange(rows)) % (2 * length)) / (2 * length)
    weight = np.full((blocks + 1, 1), 2.0)
    weight[0] = weight[blocks] = 1.0
    weight = weight * length ** -0.5 / (2 * length)
    turns = np.stack([np.cos(angle), np.sin(angle), np.cos(angle) * weight, np.sin(angle) * weight])
    angle = 2 * np.pi * (np.outer(np.arange(rows), np.arange(rows)) % rows) / rows
    cosine, sine = np.cos(angle), np.sin(angle)
    matrix = np.block([[cosine, -sine], [sine, cosine]]).astype(np.float32)
    return turns.astype(np.float32), matrix


def two_terms(value):
    high = value.astype(jnp.bfloat16)
    return high, (value - high.astype(jnp.float32)).astype(jnp.bfloat16)


def product(left, right, right_dim):
    def dot(a, b):
        return lax.dot_general(a, b, (((1,), (right_dim,)), ((), ())), preferred_element_type=jnp.float32)

    return dot(left[0], right[0]) + (dot(left[1], right[0]) + dot(left[0], right[1]))


def weighted(terms):
    total = None
    for factor, term in terms:
        if abs(factor) < 1e-12:
            continue
        if abs(factor - 1) < 1e-12:
            total = term if total is None else total + term
        elif abs(factor + 1) < 1e-12:
            total = -term if total is None else total - term
        else:
            total = factor * term if total is None else total + factor * term
    return total


def block_spectrum(x):
    blocks = len(x)
    half = blocks // 2
    plus = {p: x[p] + x[blocks - p] for p in range(1, half)}
    minus = {p: x[p] - x[blocks - p] for p in range(1, half)}
    out = []
    for a in range(blocks + 1):
        even, odd = (plus, minus) if a % 2 == 0 else (minus, plus)
        angle = [np.pi * ((p * a) % (2 * blocks)) / blocks for p in range(half + 1)]
        real = [(1.0, x[0])] + [(np.cos(angle[p]), even[p]) for p in range(1, half)]
        real.append((np.cos(angle[half]), x[half]))
        imag = [(-np.sin(angle[p]), odd[p]) for p in range(1, half)]
        imag.append((-np.sin(angle[half]), x[half]))
        out.append((weighted(real), weighted(imag)))
    return out


def block_signal(y):
    blocks = len(y) - 1
    half = blocks // 2
    out = [None] * blocks
    for p in range(half + 1):
        sums = []
        for part, wave in ((0, np.cos), (1, np.sin)):
            for parity in (0, 1):
                sums.append(weighted([
                    (wave(np.pi * ((p * a) % (2 * blocks)) / blocks), y[a][part])
                    for a in range(parity, blocks + 1, 2)
                    if y[a][part] is not None
                ]))
        signs = (1.0, 1.0, -1.0, -1.0)
        out[p] = weighted([(s, v) for s, v in zip(signs, sums) if v is not None])
        if 0 < p < half:
            signs = (1.0, -1.0, 1.0, -1.0)
            out[blocks - p] = weighted([(s, v) for s, v in zip(signs, sums) if v is not None])
    return out


def relay_kernel(
    n, sections,
    x_hbm, gate_hbm, saved_hbm, incoming_hbm, filter_hbm, skip_hbm, wv_hbm, wg_hbm, turn_hbm, matrix_hbm,
    out_ref,
    x_ref, gate_ref, saved_ref, incoming_ref, filter_ref, skip_ref, wv_ref, wg_ref, turn_ref, matrix_ref,
    load_sem,
    source, held, spec, scaled, result, back, passed, received, weight,
    send_sem, recv_sem, back_send, back_recv, hop_send, hop_recv, ready,
):
    me = lax.axis_index("seq")
    section = lax.axis_index("section")
    rows = x_ref.shape[1]
    per = held.shape[2]
    core = lax.rem(me, 2)
    partner = me + 1 - 2 * core
    below = lax.rem(section + sections - 1, sections)
    above = lax.rem(section + 1, sections)

    chip = me // 2
    last = chip == n // 2 - 1
    first = n // 4 + 1
    early = (chip < first).astype(jnp.int32)

    pairs = (
        (incoming_hbm, incoming_ref), (gate_hbm, gate_ref), (filter_hbm, filter_ref), (x_hbm, x_ref),
        (saved_hbm, saved_ref), (wg_hbm, wg_ref), (matrix_hbm, matrix_ref), (turn_hbm, turn_ref),
        (wv_hbm, wv_ref), (skip_hbm, skip_ref),
    )
    loads = [pltpu.make_async_copy(src, dst, load_sem.at[i]) for i, (src, dst) in enumerate(pairs)]

    barrier = pltpu.get_barrier_semaphore()

    def tell(semaphore, **to):
        pl.semaphore_signal(semaphore, inc=1, device_id=to, device_id_type=pl.DeviceIdType.MESH)

    for i in range(1, n // 2):
        tell(barrier, seq=2 * lax.rem(chip + i, n // 2) + 1 - early)
    tell(barrier, seq=partner)
    for neighbour in (below, above):
        tell(barrier, seq=2 * chip + 1, section=neighbour)
    for load in loads:
        load.start()

    def hear_first():
        @pl.when(core == 0)
        def _():
            pl.semaphore_wait(barrier, 2 * (first - early) + 1)
            tell(ready.at[0], seq=partner)

        @pl.when(core == 1)
        def _():
            pl.semaphore_wait(ready.at[0], 1)

    def hear_rest():
        @pl.when(core == 1)
        def _():
            pl.semaphore_wait(barrier, 2 * (n // 2 - first - 1 + early) + 5)
            tell(ready.at[1], seq=partner)
            tell(ready.at[2], seq=me, section=above)
            tell(ready.at[2], seq=partner, section=above)

        @pl.when(core == 0)
        def _():
            pl.semaphore_wait(ready.at[1], 1)

    def each(places, act):
        for p in places:
            pl.when(p != me)(functools.partial(act, p))

    def out_copy(signal, to):
        return pltpu.make_async_remote_copy(
            src_ref=source.at[signal, pl.ds(pl.multiple_of(to * per, 8), per)],
            dst_ref=held.at[signal, me],
            send_sem=send_sem.at[signal, to],
            recv_sem=recv_sem.at[signal, me],
            device_id={"seq": to},
            device_id_type=pl.DeviceIdType.MESH,
        )

    def out_arrival(signal, origin):
        return pltpu.make_async_remote_copy(
            src_ref=source.at[signal, pl.ds(0, per)],
            dst_ref=held.at[signal, origin],
            send_sem=send_sem.at[signal, origin],
            recv_sem=recv_sem.at[signal, origin],
            device_id={"seq": origin},
            device_id_type=pl.DeviceIdType.MESH,
        )

    def back_copy(which, to):
        return pltpu.make_async_remote_copy(
            src_ref=result.at[which, to],
            dst_ref=back.at[which, pl.ds(pl.multiple_of(me * per, 8), per)],
            send_sem=back_send.at[which, to],
            recv_sem=back_recv.at[which, me],
            device_id={"seq": to, "section": section if which else below},
            device_id_type=pl.DeviceIdType.MESH,
        )

    def back_arrival(which, origin):
        return pltpu.make_async_remote_copy(
            src_ref=result.at[which, origin],
            dst_ref=back.at[which, pl.ds(pl.multiple_of(origin * per, 8), per)],
            send_sem=back_send.at[which, origin],
            recv_sem=back_recv.at[which, origin],
            device_id={"seq": origin, "section": section if which else below},
            device_id_type=pl.DeviceIdType.MESH,
        )

    def hop_copy(which, src, dst):
        return pltpu.make_async_remote_copy(
            src_ref=src,
            dst_ref=dst,
            send_sem=hop_send.at[which],
            recv_sem=hop_recv.at[which],
            device_id={"section": below},
            device_id_type=pl.DeviceIdType.MESH,
        )

    part = weight.shape[1] // 2
    half = pl.ds(pl.multiple_of(core * part, 8), part)
    weight_hop = hop_copy(0, wv_hbm.at[:, half], weight.at[:, half])
    weight_share = pltpu.make_async_remote_copy(
        src_ref=weight.at[:, half],
        dst_ref=weight.at[:, half],
        send_sem=hop_send.at[2],
        recv_sem=hop_recv.at[2],
        device_id={"seq": partner},
        device_id_type=pl.DeviceIdType.MESH,
    )
    passed_hop = hop_copy(1, passed, received)
    mine = pl.ds(pl.multiple_of(me * per, 8), per)
    soon, late = range(2 * first), range(2 * first, n)

    def send(signal, places):
        each(places, lambda to: out_copy(signal, to).start())

    loads[0].wait()
    loads[1].wait()
    source[2] = (incoming_ref[0] * gate_ref[0]).T
    hear_first()
    send(2, soon)
    loads[2].wait()
    source[0] = filter_ref[0].T
    send(0, soon)
    loads[3].wait()
    source[1] = x_ref[0].T
    hear_rest()
    send(2, late)
    send(0, late)
    weight_hop.start()


    @pl.when(last)
    def _():
        send(1, range(n // 2, n))
        each(range(n // 2), lambda to: out_copy(0, to).wait_send())
        send(1, range(n // 2))

    @pl.when(chip == 0)
    def _():
        send(1, range(n // 2))
        each(range(n // 2, n), lambda to: out_copy(0, to).wait_send())
        send(1, range(n // 2, n))

    @pl.when(jnp.logical_not(last | (chip == 0)))
    def _():
        send(1, range(n))

    for signal in range(3):
        held[signal, me] = source[signal, mine]

    for load in loads[4:]:
        load.wait()
    passed[...] = product(two_terms(incoming_ref[0] * saved_ref[0]), two_terms(wg_ref[0]), 1) + product(
        two_terms(skip_ref[...] * (incoming_ref[0] * gate_ref[0])), two_terms(wv_ref[0]), 1
    )
    passed_hop.start()
    matrix = two_terms(matrix_ref[...])

    def forward(signal, wait=True):
        if wait:
            each(range(n), lambda origin: out_arrival(signal, origin).wait_recv())
        for a, (real, imag) in enumerate(block_spectrum([held[signal, p] for p in range(n)])):
            at = pl.ds(a * per, per)
            if a == 0:
                scaled[at, :rows] = real
                scaled[at, rows:] = jnp.zeros_like(real)
                continue
            cosine, sine = turn_ref[0, a : a + 1], turn_ref[1, a : a + 1]
            if imag is None:
                scaled[at, :rows] = real * cosine
                scaled[at, rows:] = -real * sine
            else:
                scaled[at, :rows] = real * cosine + imag * sine
                scaled[at, rows:] = imag * cosine - real * sine
        spec[signal] = product(two_terms(scaled[...]), matrix, 0)

    def inverse(which):
        kr, ki = spec[which, :, :rows], spec[which, :, rows:]
        gr, gi = spec[2, :, :rows], spec[2, :, rows:]
        scaled[:, :rows] = kr * gr + ki * gi
        scaled[:, rows:] = kr * gi - ki * gr
        scaled[...] = product(two_terms(scaled[...]), matrix, 1)
        terms = []
        for a in range(n + 1):
            at = pl.ds(a * per, per)
            real, imag = scaled[at, :rows], scaled[at, rows:]
            cosine, sine = turn_ref[2, a : a + 1], turn_ref[3, a : a + 1]
            if a == 0:
                terms.append((real * cosine, None))
            elif a == n:
                terms.append((real * cosine - imag * sine, None))
            else:
                terms.append((real * cosine - imag * sine, real * sine + imag * cosine))
        for p, value in enumerate(block_signal(terms)):
            result[which, p] = value
        near, middle = range(n // 4), range(n // 4, n // 2)
        if which:
            @pl.when(last)
            def _():
                each(near, lambda to: back_copy(1, to).start())
                each(near, lambda to: back_copy(1, to).wait_send())
                each(range(n // 4, n), lambda to: back_copy(1, to).start())

            @pl.when(jnp.logical_not(last))
            def _():
                each(range(n), lambda to: back_copy(1, to).start())
        else:
            pl.semaphore_wait(ready.at[2], 1)

            @pl.when(last)
            def _():
                for to in [*near, *range(n // 2, n)]:
                    back_copy(0, to).start()

            @pl.when(jnp.logical_not(last))
            def _():
                for to in range(n):
                    back_copy(0, to).start()

    forward(2)
    forward(0)
    inverse(0)
    weight_hop.wait_recv()
    weight_share.start()
    each(range(n), lambda origin: out_arrival(1, origin).wait_recv())

    @pl.when(last)
    def _():
        for to in range(n // 4, n // 2):
            back_copy(0, to).start()

    forward(1, False)
    inverse(1)

    back[1, mine] = result[1, me]
    passed_hop.wait_recv()
    weight_share.wait_recv()
    w_above = two_terms(weight[0])
    for origin in range(n):
        back_arrival(0, origin).wait_recv()
    out_ref[0] = product(two_terms(back[0].T), w_above, 1) + received[...]
    each(range(n), lambda origin: back_arrival(1, origin).wait_recv())
    out_ref[1] = back[1].T
    for signal in (1, 2):
        each(range(n), lambda to: out_copy(signal, to).wait_send())

    @pl.when(last)
    def _():
        each(range(n // 2, n), lambda to: out_copy(0, to).wait_send())

    @pl.when(chip == 0)
    def _():
        each(range(n // 2), lambda to: out_copy(0, to).wait_send())

    @pl.when(jnp.logical_not(last | (chip == 0)))
    def _():
        each(range(n), lambda to: out_copy(0, to).wait_send())

    each(range(n // 4, n), lambda to: back_copy(1, to).wait_send())

    @pl.when(jnp.logical_not(last))
    def _():
        each(range(n // 4), lambda to: back_copy(1, to).wait_send())

    for to in range(n):
        back_copy(0, to).wait_send()
    weight_hop.wait_send()
    weight_share.wait_send()
    passed_hop.wait_send()


def in_one_kernel(*operands):
    n, sections = lax.axis_size("seq"), lax.axis_size("section")
    _, rows, channels = operands[0].shape
    per = channels // n
    turns, matrix = turn_tables(n, rows)
    vmem = pl.BlockSpec(memory_space=pltpu.VMEM)
    shape = pltpu.VMEM(operands[0].shape, jnp.float32)
    spectrum = ((n + 1) * per, 2 * rows)
    dma = pltpu.SemaphoreType.DMA
    return pl.pallas_call(
        functools.partial(relay_kernel, n, sections),
        out_shape=pltpu.VMEM((2,) + operands[0].shape[1:], jnp.float32),
        in_specs=[pl.BlockSpec(memory_space=pltpu.HBM)] * 10,
        out_specs=vmem,
        scratch_shapes=[
            *(pltpu.VMEM(operand.shape, jnp.float32) for operand in operands + (turns, matrix)),
            dma((10,)),
            pltpu.VMEM((3, channels, rows), jnp.float32),
            pltpu.VMEM((3, n, per, rows), jnp.float32),
            pltpu.VMEM((3,) + spectrum, jnp.float32),
            pltpu.VMEM(spectrum, jnp.float32),
            pltpu.VMEM((2, n, per, rows), jnp.float32),
            pltpu.VMEM((2, channels, rows), jnp.float32),
            pltpu.VMEM((rows, channels), jnp.float32),
            pltpu.VMEM((rows, channels), jnp.float32),
            pltpu.VMEM((1, channels, channels), jnp.float32),
            dma((3, n)), dma((3, n)),
            dma((2, n)), dma((2, n)),
            dma((3,)), dma((3,)),
            pltpu.SemaphoreType.REGULAR((3,)),
        ],
        compiler_params=pltpu.CompilerParams(
            collective_id=0, has_side_effects=True, vmem_limit_bytes=60 * 2**20
        ),
    )(*operands, turns, matrix)


def per_device(*operands):
    n, sections = lax.axis_size("seq"), lax.axis_size("section")
    _, rows, channels = operands[0].shape
    if sections > 1 and channels % (8 * n) == 0 and n % 2 == 0 and rows % 128 == 0:
        both = in_one_kernel(*operands)
        return both[:1], both[1:]
    return spread_out(*operands)


def solution(mesh):
    in_specs = (
        P("section", "seq", None),
        P("section", "seq", None),
        P("section", "seq", None),
        P("section", "seq", None),
        P("section", "seq", None),
        P("section", None),
        P("section", None, None),
        P("section", None, None),
    )
    out_specs = (P("section", "seq", None), P("section", "seq", None))
    return jax.shard_map(
        per_device, mesh=mesh, in_specs=in_specs, out_specs=out_specs, check_vma=False
    )
```

```python
import functools

import jax
import jax.numpy as jnp
import numpy as np
from jax import lax
from jax.experimental import pallas as pl
from jax.experimental.pallas import tpu as pltpu
from jax.sharding import PartitionSpec as P

exact_mode = lax.Precision.HIGHEST
full_turn = 6.283185307179586


def passed_along(block, axis, distance):
    devices = range(lax.axis_size(axis))
    route = [((i - distance) % len(devices), i) for i in devices]
    return lax.ppermute(block, axis, route)


def rotations(left_index, right_index, period):
    product = left_index[:, None] * right_index[None, :] % period
    phases = product.astype(jnp.float32) * (full_turn / period)
    return (jnp.cos(phases), jnp.sin(phases))


def across_blocks(signals):
    blocks = signals.shape[1]
    cosine, sine_part = rotations(jnp.arange(2 * blocks), jnp.arange(blocks), 2 * blocks)
    tables = jnp.stack([cosine, -sine_part])
    parts = jnp.einsum("akq,sqrc->askrc", tables, signals, precision=exact_mode)
    return (parts[0], parts[1])


def twiddle(real_part, imag_part, row_index, frequency, period, direction):
    cosine, sine_part = rotations(frequency, row_index, period)
    cosine = cosine[None, :, :, None]
    sine_part = direction * sine_part[None, :, :, None]
    new_real = real_part * cosine + imag_part * sine_part
    new_imag = imag_part * cosine - real_part * sine_part
    return (new_real, new_imag)


def along_rows(real_part, imag_part, direction):
    row_count = real_part.shape[2]
    positions = jnp.arange(row_count)
    cosine, sine_part = rotations(positions, positions, row_count)
    tables = jnp.stack([cosine, direction * sine_part])
    paired = jnp.stack([real_part, imag_part])
    terms = jnp.einsum("ajr,bskrc->abskjc", tables, paired, precision=exact_mode)
    return (terms[0, 0] + terms[1, 1], terms[0, 1] - terms[1, 0])


def inverse_blocks(real_part, imag_part):
    frequency = real_part.shape[1]
    blocks = frequency // 2
    cosine, sine_part = rotations(jnp.arange(blocks), jnp.arange(frequency), frequency)
    first_term = jnp.einsum("qk,skrc->sqrc", cosine, real_part, precision=exact_mode)
    second_term = jnp.einsum("qk,skrc->sqrc", sine_part, imag_part, precision=exact_mode)
    return first_term - second_term


def spectrum_rows(signals):
    devices = lax.axis_size("seq")
    position = lax.axis_index("seq")
    row_count = signals.shape[1]
    slice_rows = row_count // devices
    regrouped = lax.all_to_all(signals, "seq", split_axis=1, concat_axis=1, tiled=True)
    regrouped = regrouped.reshape(signals.shape[0], devices, slice_rows, signals.shape[2])
    real_part, imag_part = across_blocks(regrouped)
    row_index = position * slice_rows + jnp.arange(slice_rows)
    real_part, imag_part = twiddle(
        real_part, imag_part, row_index, jnp.arange(2 * devices), 2 * devices * row_count, 1.0
    )
    complex_pair = lax.all_to_all(
        jnp.stack([real_part, imag_part]), "seq", split_axis=2, concat_axis=3, tiled=True
    )
    return along_rows(complex_pair[0], complex_pair[1], 1.0)


def signal_rows(real_part, imag_part):
    devices = lax.axis_size("seq")
    position = lax.axis_index("seq")
    row_count = real_part.shape[2]
    real_part, imag_part = along_rows(real_part, imag_part, -1.0)
    frequency = position * 2 + jnp.arange(2)
    real_part, imag_part = twiddle(
        real_part, imag_part, jnp.arange(row_count), frequency, 2 * devices * row_count, -1.0
    )
    complex_pair = lax.all_to_all(
        jnp.stack([real_part, imag_part]), "seq", split_axis=3, concat_axis=2, tiled=True
    )
    values = inverse_blocks(complex_pair[0], complex_pair[1])
    regrouped = lax.all_to_all(values, "seq", split_axis=1, concat_axis=2, tiled=True)
    regrouped = regrouped.reshape(values.shape[0], row_count, values.shape[3])
    return regrouped / (2 * devices * row_count)


def correlate(kernel_real, kernel_imag, grad_real, grad_imag):
    product_real = kernel_real * grad_real + kernel_imag * grad_imag
    product_imag = kernel_real * grad_imag - kernel_imag * grad_real
    return (product_real, product_imag)


def spread_out(conv_input, gate, conv_out, incoming, filter_raw, skip_gain, w_value, w_gate):
    row_count = conv_input.shape[1]
    devices = lax.axis_size("seq")
    filter_scale = (devices * row_count) ** (-0.5)
    kernel = filter_raw[0] * filter_scale
    conv_grad = incoming[0] * gate[0]
    gate_grad = incoming[0] * conv_out[0]
    known_real, known_imag = spectrum_rows(jnp.stack([kernel, conv_input[0]]))
    grad_real, grad_imag = spectrum_rows(conv_grad[None])
    product_real, product_imag = correlate(known_real, known_imag, grad_real, grad_imag)
    grads = signal_rows(product_real, product_imag)
    value_grad = grads[0] + skip_gain[0][None, :] * conv_grad
    filter_grad = grads[1] * filter_scale
    input_grad = jnp.einsum("tc,dc->td", value_grad, w_value[0], precision=exact_mode)
    input_grad = input_grad + jnp.einsum("tc,dc->td", gate_grad, w_gate[0], precision=exact_mode)
    handed = passed_along(input_grad, "section", -1)
    return (handed[None], filter_grad[None])


def turn_tables(blocks, rows):
    length = blocks * rows
    angle = 2 * np.pi * (np.outer(np.arange(blocks + 1), np.arange(rows)) % (2 * length)) / (2 * length)
    weight = np.full((blocks + 1, 1), 2.0)
    weight[0] = weight[blocks] = 1.0
    weight = weight * length ** -0.5 / (2 * length)
    turns = np.stack([np.cos(angle), np.sin(angle), np.cos(angle) * weight, np.sin(angle) * weight])
    angle = 2 * np.pi * (np.outer(np.arange(rows), np.arange(rows)) % rows) / rows
    cosine, sine = np.cos(angle), np.sin(angle)
    matrix = np.block([[cosine, -sine], [sine, cosine]]).astype(np.float32)
    return turns.astype(np.float32), matrix


def two_terms(value):
    high = value.astype(jnp.bfloat16)
    return high, (value - high.astype(jnp.float32)).astype(jnp.bfloat16)


def product(left, right, right_dim):
    def dot(a, b):
        return lax.dot_general(a, b, (((1,), (right_dim,)), ((), ())), preferred_element_type=jnp.float32)

    return dot(left[0], right[0]) + (dot(left[1], right[0]) + dot(left[0], right[1]))


def weighted(terms):
    total = None
    for factor, term in terms:
        if abs(factor) < 1e-12:
            continue
        if abs(factor - 1) < 1e-12:
            total = term if total is None else total + term
        elif abs(factor + 1) < 1e-12:
            total = -term if total is None else total - term
        else:
            total = factor * term if total is None else total + factor * term
    return total


def block_spectrum(x):
    blocks = len(x)
    half = blocks // 2
    plus = {p: x[p] + x[blocks - p] for p in range(1, half)}
    minus = {p: x[p] - x[blocks - p] for p in range(1, half)}
    out = []
    for a in range(blocks + 1):
        even, odd = (plus, minus) if a % 2 == 0 else (minus, plus)
        angle = [np.pi * ((p * a) % (2 * blocks)) / blocks for p in range(half + 1)]
        real = [(1.0, x[0])] + [(np.cos(angle[p]), even[p]) for p in range(1, half)]
        real.append((np.cos(angle[half]), x[half]))
        imag = [(-np.sin(angle[p]), odd[p]) for p in range(1, half)]
        imag.append((-np.sin(angle[half]), x[half]))
        out.append((weighted(real), weighted(imag)))
    return out


def block_signal(y):
    blocks = len(y) - 1
    half = blocks // 2
    out = [None] * blocks
    for p in range(half + 1):
        sums = []
        for part, wave in ((0, np.cos), (1, np.sin)):
            for parity in (0, 1):
                sums.append(weighted([
                    (wave(np.pi * ((p * a) % (2 * blocks)) / blocks), y[a][part])
                    for a in range(parity, blocks + 1, 2)
                    if y[a][part] is not None
                ]))
        signs = (1.0, 1.0, -1.0, -1.0)
        out[p] = weighted([(s, v) for s, v in zip(signs, sums) if v is not None])
        if 0 < p < half:
            signs = (1.0, -1.0, 1.0, -1.0)
            out[blocks - p] = weighted([(s, v) for s, v in zip(signs, sums) if v is not None])
    return out


def relay_kernel(
    n, sections,
    x_hbm, gate_hbm, saved_hbm, incoming_hbm, filter_hbm, skip_hbm, wv_hbm, wg_hbm, turn_hbm, matrix_hbm,
    out_ref,
    x_ref, gate_ref, saved_ref, incoming_ref, filter_ref, skip_ref, wv_ref, wg_ref, turn_ref, matrix_ref,
    load_sem,
    source, held, spec, scaled, result, back, passed, received, weight,
    send_sem, recv_sem, back_send, back_recv, hop_send, hop_recv, ready,
):
    me = lax.axis_index("seq")
    section = lax.axis_index("section")
    rows = x_ref.shape[1]
    per = held.shape[2]
    core = lax.rem(me, 2)
    partner = me + 1 - 2 * core
    below = lax.rem(section + sections - 1, sections)
    above = lax.rem(section + 1, sections)

    chip = me // 2
    last = chip == n // 2 - 1
    first = n // 4 + 1
    early = (chip < first).astype(jnp.int32)

    pairs = (
        (incoming_hbm, incoming_ref), (gate_hbm, gate_ref), (filter_hbm, filter_ref), (x_hbm, x_ref),
        (saved_hbm, saved_ref), (wg_hbm, wg_ref), (matrix_hbm, matrix_ref), (turn_hbm, turn_ref),
        (wv_hbm, wv_ref), (skip_hbm, skip_ref),
    )
    loads = [pltpu.make_async_copy(src, dst, load_sem.at[i]) for i, (src, dst) in enumerate(pairs)]

    for load in loads[:2]:
        load.start()
    barrier = pltpu.get_barrier_semaphore()

    def tell(semaphore, **to):
        pl.semaphore_signal(semaphore, inc=1, device_id=to, device_id_type=pl.DeviceIdType.MESH)

    for i in range(1, n // 2):
        tell(barrier, seq=2 * lax.rem(chip + n // 2 - i, n // 2) + 1 - early)
    tell(barrier, seq=partner)
    for neighbour in (below, above):
        tell(barrier, seq=2 * chip + 1, section=neighbour)
    for load in loads[2:]:
        load.start()

    def hear_first():
        @pl.when(core == 0)
        def _():
            pl.semaphore_wait(barrier, 2 * (first - early) + 1)
            tell(ready.at[0], seq=partner)

        @pl.when(core == 1)
        def _():
            pl.semaphore_wait(ready.at[0], 1)

    def hear_rest():
        @pl.when(core == 1)
        def _():
            pl.semaphore_wait(barrier, 2 * (n // 2 - first - 1 + early) + 5)
            tell(ready.at[1], seq=partner)
            tell(ready.at[2], seq=me, section=above)
            tell(ready.at[2], seq=partner, section=above)

        @pl.when(core == 0)
        def _():
            pl.semaphore_wait(ready.at[1], 1)

    def each(places, act):
        for p in places:
            pl.when(p != me)(functools.partial(act, p))

    def out_copy(signal, to):
        return pltpu.make_async_remote_copy(
            src_ref=source.at[signal, pl.ds(pl.multiple_of(to * per, 8), per)],
            dst_ref=held.at[signal, me],
            send_sem=send_sem.at[signal, to],
            recv_sem=recv_sem.at[signal, me],
            device_id={"seq": to},
            device_id_type=pl.DeviceIdType.MESH,
        )

    def out_arrival(signal, origin):
        return pltpu.make_async_remote_copy(
            src_ref=source.at[signal, pl.ds(0, per)],
            dst_ref=held.at[signal, origin],
            send_sem=send_sem.at[signal, origin],
            recv_sem=recv_sem.at[signal, origin],
            device_id={"seq": origin},
            device_id_type=pl.DeviceIdType.MESH,
        )

    def back_copy(which, to):
        return pltpu.make_async_remote_copy(
            src_ref=result.at[which, to],
            dst_ref=back.at[which, pl.ds(pl.multiple_of(me * per, 8), per)],
            send_sem=back_send.at[which, to],
            recv_sem=back_recv.at[which, me],
            device_id={"seq": to, "section": section if which else below},
            device_id_type=pl.DeviceIdType.MESH,
        )

    def back_arrival(which, origin):
        return pltpu.make_async_remote_copy(
            src_ref=result.at[which, origin],
            dst_ref=back.at[which, pl.ds(pl.multiple_of(origin * per, 8), per)],
            send_sem=back_send.at[which, origin],
            recv_sem=back_recv.at[which, origin],
            device_id={"seq": origin, "section": section if which else below},
            device_id_type=pl.DeviceIdType.MESH,
        )

    def hop_copy(which, src, dst):
        return pltpu.make_async_remote_copy(
            src_ref=src,
            dst_ref=dst,
            send_sem=hop_send.at[which],
            recv_sem=hop_recv.at[which],
            device_id={"section": below},
            device_id_type=pl.DeviceIdType.MESH,
        )

    part = weight.shape[1] // 2
    half = pl.ds(pl.multiple_of(core * part, 8), part)
    weight_hop = hop_copy(0, wv_hbm.at[:, half], weight.at[:, half])
    weight_share = pltpu.make_async_remote_copy(
        src_ref=weight.at[:, half],
        dst_ref=weight.at[:, half],
        send_sem=hop_send.at[2],
        recv_sem=hop_recv.at[2],
        device_id={"seq": partner},
        device_id_type=pl.DeviceIdType.MESH,
    )
    passed_hop = hop_copy(1, passed, received)
    mine = pl.ds(pl.multiple_of(me * per, 8), per)
    soon, late = range(2 * first), range(2 * first, n)

    def send(signal, places):
        each(places, lambda to: out_copy(signal, to).start())

    loads[0].wait()
    loads[1].wait()
    source[2] = (incoming_ref[0] * gate_ref[0]).T
    hear_first()
    send(2, soon)
    loads[2].wait()
    source[0] = filter_ref[0].T
    send(0, soon)
    loads[3].wait()
    source[1] = x_ref[0].T
    hear_rest()
    send(2, late)
    send(0, late)
    weight_hop.start()


    @pl.when(last)
    def _():
        send(1, range(n // 2, n))
        each(range(n // 2), lambda to: out_copy(0, to).wait_send())
        send(1, range(n // 2))

    @pl.when(chip == 0)
    def _():
        send(1, range(n // 2))
        each(range(n // 2, n), lambda to: out_copy(0, to).wait_send())
        send(1, range(n // 2, n))

    @pl.when(jnp.logical_not(last | (chip == 0)))
    def _():
        send(1, range(n))

    for signal in range(3):
        held[signal, me] = source[signal, mine]

    for load in loads[4:]:
        load.wait()
    passed[...] = product(two_terms(incoming_ref[0] * saved_ref[0]), two_terms(wg_ref[0]), 1) + product(
        two_terms(skip_ref[...] * (incoming_ref[0] * gate_ref[0])), two_terms(wv_ref[0]), 1
    )
    passed_hop.start()
    matrix = two_terms(matrix_ref[...])

    def forward(signal, wait=True):
        if wait:
            each(range(n), lambda origin: out_arrival(signal, origin).wait_recv())
        for a, (real, imag) in enumerate(block_spectrum([held[signal, p] for p in range(n)])):
            at = pl.ds(a * per, per)
            if a == 0:
                scaled[at, :rows] = real
                scaled[at, rows:] = jnp.zeros_like(real)
                continue
            cosine, sine = turn_ref[0, a : a + 1], turn_ref[1, a : a + 1]
            if imag is None:
                scaled[at, :rows] = real * cosine
                scaled[at, rows:] = -real * sine
            else:
                scaled[at, :rows] = real * cosine + imag * sine
                scaled[at, rows:] = imag * cosine - real * sine
        spec[signal] = product(two_terms(scaled[...]), matrix, 0)

    near, middle = range(n // 4), range(n // 4, n // 2)

    def inverse(which):
        kr, ki = spec[which, :, :rows], spec[which, :, rows:]
        gr, gi = spec[2, :, :rows], spec[2, :, rows:]
        scaled[:, :rows] = kr * gr + ki * gi
        scaled[:, rows:] = kr * gi - ki * gr
        scaled[...] = product(two_terms(scaled[...]), matrix, 1)
        terms = []
        for a in range(n + 1):
            at = pl.ds(a * per, per)
            real, imag = scaled[at, :rows], scaled[at, rows:]
            cosine, sine = turn_ref[2, a : a + 1], turn_ref[3, a : a + 1]
            if a == 0:
                terms.append((real * cosine, None))
            elif a == n:
                terms.append((real * cosine - imag * sine, None))
            else:
                terms.append((real * cosine - imag * sine, real * sine + imag * cosine))
        for p, value in enumerate(block_signal(terms)):
            result[which, p] = value
            if p == n // 4 - 1:
                if which:
                    each(near, lambda to: back_copy(1, to).start())
                else:
                    for to in near:
                        back_copy(0, to).start()

        if which:
            @pl.when(last)
            def _():
                each(near, lambda to: back_copy(1, to).wait_send())

            each(range(n // 4, n), lambda to: back_copy(1, to).start())
        else:
            @pl.when(jnp.logical_not(last))
            def _():
                for to in middle:
                    back_copy(0, to).start()

            for to in range(n // 2, n):
                back_copy(0, to).start()

    forward(2)
    pl.semaphore_wait(ready.at[2], 1)
    forward(0)
    inverse(0)
    weight_hop.wait_recv()
    weight_share.start()
    each(range(n), lambda origin: out_arrival(1, origin).wait_recv())

    @pl.when(last)
    def _():
        for to in middle:
            back_copy(0, to).start()

    forward(1, False)
    inverse(1)

    back[1, mine] = result[1, me]
    passed_hop.wait_recv()
    weight_share.wait_recv()
    w_above = two_terms(weight[0])
    for origin in range(n):
        back_arrival(0, origin).wait_recv()
    out_ref[0] = product(two_terms(back[0].T), w_above, 1) + received[...]
    for signal in (1, 2):
        each(range(n), lambda to: out_copy(signal, to).wait_send())

    @pl.when(last)
    def _():
        each(range(n // 2, n), lambda to: out_copy(0, to).wait_send())

    @pl.when(chip == 0)
    def _():
        each(range(n // 2), lambda to: out_copy(0, to).wait_send())

    @pl.when(jnp.logical_not(last | (chip == 0)))
    def _():
        each(range(n), lambda to: out_copy(0, to).wait_send())

    for to in range(n):
        back_copy(0, to).wait_send()
    lower, cut = range(n // 2), back.shape[1] // 2
    each(lower, lambda origin: back_arrival(1, origin).wait_recv())
    out_ref[1, :, :cut] = back[1, :cut].T
    each(range(n // 2, n), lambda origin: back_arrival(1, origin).wait_recv())
    out_ref[1, :, cut:] = back[1, cut:].T
    each(range(n // 4, n), lambda to: back_copy(1, to).wait_send())

    @pl.when(jnp.logical_not(last))
    def _():
        each(range(n // 4), lambda to: back_copy(1, to).wait_send())

    weight_hop.wait_send()
    weight_share.wait_send()
    passed_hop.wait_send()


def in_one_kernel(*operands):
    n, sections = lax.axis_size("seq"), lax.axis_size("section")
    _, rows, channels = operands[0].shape
    per = channels // n
    turns, matrix = turn_tables(n, rows)
    vmem = pl.BlockSpec(memory_space=pltpu.VMEM)
    shape = pltpu.VMEM(operands[0].shape, jnp.float32)
    spectrum = ((n + 1) * per, 2 * rows)
    dma = pltpu.SemaphoreType.DMA
    return pl.pallas_call(
        functools.partial(relay_kernel, n, sections),
        out_shape=pltpu.VMEM((2,) + operands[0].shape[1:], jnp.float32),
        in_specs=[pl.BlockSpec(memory_space=pltpu.HBM)] * 10,
        out_specs=vmem,
        scratch_shapes=[
            *(pltpu.VMEM(operand.shape, jnp.float32) for operand in operands + (turns, matrix)),
            dma((10,)),
            pltpu.VMEM((3, channels, rows), jnp.float32),
            pltpu.VMEM((3, n, per, rows), jnp.float32),
            pltpu.VMEM((3,) + spectrum, jnp.float32),
            pltpu.VMEM(spectrum, jnp.float32),
            pltpu.VMEM((2, n, per, rows), jnp.float32),
            pltpu.VMEM((2, channels, rows), jnp.float32),
            pltpu.VMEM((rows, channels), jnp.float32),
            pltpu.VMEM((rows, channels), jnp.float32),
            pltpu.VMEM((1, channels, channels), jnp.float32),
            dma((3, n)), dma((3, n)),
            dma((2, n)), dma((2, n)),
            dma((3,)), dma((3,)),
            pltpu.SemaphoreType.REGULAR((3,)),
        ],
        compiler_params=pltpu.CompilerParams(
            collective_id=0, has_side_effects=True, vmem_limit_bytes=60 * 2**20
        ),
    )(*operands, turns, matrix)


def per_device(*operands):
    n, sections = lax.axis_size("seq"), lax.axis_size("section")
    _, rows, channels = operands[0].shape
    if sections > 1 and channels % (8 * n) == 0 and n % 2 == 0 and rows % 128 == 0:
        both = in_one_kernel(*operands)
        return both[:1], both[1:]
    return spread_out(*operands)


def solution(mesh):
    in_specs = (
        P("section", "seq", None),
        P("section", "seq", None),
        P("section", "seq", None),
        P("section", "seq", None),
        P("section", "seq", None),
        P("section", None),
        P("section", None, None),
        P("section", None, None),
    )
    out_specs = (P("section", "seq", None), P("section", "seq", None))
    return jax.shard_map(
        per_device, mesh=mesh, in_specs=in_specs, out_specs=out_specs, check_vma=False
    )
```
